128 devices in a mesh: org: 16 (over y, x), dst: 8 (over z, core).
Axes of the slice: x: 4, y: 4, z: 4, core: 2. Of those that a mesh axis runs over, the one named last changes fastest.
Arguments:
- counts: int32 [8, 8192, 8192], P(None, 'org', 'dst'), may hold values from 0 to 127, as said below
- block_scales: float32 [8, 64, 64], P(None, 'org', 'dst'), may hold values from 0.05 to 12.5, as said below
- anchor_factor: float32 [64, 8192], P(None, 'org'), may hold values from 0.2 to 9, as said below
- dest_factor: float32 [64, 8192], P(None, 'dst'), may hold values from 0.2 to 9, as said below
- hour_factor: float32 [8, 64], replicated, may hold values from 0.5 to 2
Outputs:
- anchor_updated: float32 [64, 8192], P(None, 'org')
- dest_updated: float32 [64, 8192], P(None, 'dst')
The draws below stay inside these ranges and needn't reach their ends.
Inputs may be any that keep to these rules, and one draw needn't show every extreme that they name: Whole trip counts. `block_scales`: positive. `anchor_factor`: positive. `dest_factor`: positive.
All inputs are finite; a program needn't handle non-finite values.
Results may differ from the reference program's by a relative error of at most 0.0003.
Values sent between devices are 32-bit elements; how exact they have to be, the bound alone decides.
A program may use at most 128 MiB of HBM per device.

```python
import math
import jax
import jax.numpy as jnp
from jax import lax

RANK = 64
HOURS = 8
SCALE_BLOCK = 128
SWEEPS = 6
ANCHORS = 8192
DESTINATIONS = 8192


def ramp_factor(key, length, growth, low_end, high_end):
    uniform_part = jax.random.uniform(key, (RANK, length), jnp.float32, low_end, high_end)
    position = jnp.arange(length, dtype=jnp.float32) / (length - 1)
    return uniform_part * jnp.exp(jnp.log(growth) * position)


def draw_counts(key, part):
    components = 4
    folded = jax.random.fold_in(key, 51)
    anchor_key = jax.random.fold_in(folded, 1)
    dest_key = jax.random.fold_in(folded, 2)
    hour_key = jax.random.fold_in(folded, 3)
    jitter_key = jax.random.fold_in(folded, 4)
    anchor_mass = jax.random.randint(anchor_key, (components, ANCHORS), 0, 8, jnp.int32).at[:, 0].set(7)
    dest_mass = jax.random.randint(dest_key, (components, DESTINATIONS), 0, 8, jnp.int32).at[:, 0].set(7)
    hour_mass = jax.random.randint(hour_key, (HOURS, components), 1, 4, jnp.int32).at[0, :].set(3)
    weighted = hour_mass[:, :, None] * anchor_mass[None, :, :]
    structure = jnp.einsum('hki,kj->hij', weighted, dest_mass)
    jitter_part = jax.random.randint(jitter_key, (HOURS, ANCHORS, DESTINATIONS), 0, 32, jnp.int32)
    return jnp.clip(structure // 2 + jitter_part, 0, 127).astype(jnp.int32)


def draw_anchor_factor(key, part):
    folded = jax.random.fold_in(key, 11)
    return ramp_factor(folded, ANCHORS, 3.0, 0.5, 1.5)


def draw_dest_factor(key, part):
    folded = jax.random.fold_in(key, 37)
    return ramp_factor(folded, DESTINATIONS, 3.0, 0.5, 1.5)


def draw_block_scales(key, part):
    row_blocks = ANCHORS // SCALE_BLOCK
    col_blocks = DESTINATIONS // SCALE_BLOCK
    folded = jax.random.fold_in(key, 23)
    unit_draw = jax.random.uniform(folded, (HOURS, row_blocks, col_blocks), jnp.float32)
    low_end = 0.1
    high_end = 1.0
    growth = 3.0
    levels = jnp.exp(jnp.log(low_end) + unit_draw * jnp.log(high_end / low_end))
    row_pos = jnp.arange(row_blocks, dtype=jnp.float32) / (row_blocks - 1)
    col_pos = jnp.arange(col_blocks, dtype=jnp.float32) / (col_blocks - 1)
    ramp_both = jnp.exp(jnp.log(growth) * (row_pos[None, :, None] + col_pos[None, None, :]))
    return levels * ramp_both


def setup_inputs(seed: int = 0) -> dict:
    streams_of = jax.random.split(jax.random.key(seed), 6)
    counts = draw_counts(jax.random.fold_in(streams_of[5], 71), 0)
    block_scales = draw_block_scales(jax.random.fold_in(streams_of[5], 71), 0)
    anchor_factor = draw_anchor_factor(jax.random.fold_in(streams_of[5], 71), 0)
    dest_factor = draw_dest_factor(jax.random.fold_in(streams_of[5], 71), 0)
    hour_factor = jnp.clip(jnp.exp(jax.random.uniform(streams_of[4], (HOURS, RANK), jnp.float32, math.log(0.5), math.log(2.0))), 0.5, 2.0)
    return {"counts": counts, "block_scales": block_scales, "anchor_factor": anchor_factor, "dest_factor": dest_factor, "hour_factor": hour_factor}


def dequantize(counts_hour, scales_hour):
    row_count, col_count = counts_hour.shape
    blocks = counts_hour.reshape(row_count // SCALE_BLOCK, SCALE_BLOCK, col_count // SCALE_BLOCK, SCALE_BLOCK).astype(jnp.float32)
    values = blocks * scales_hour[:, None, :, None]
    return values.reshape(row_count, col_count).astype(jnp.bfloat16)


def gram_matrix(factor, hour_gram):
    return jnp.dot(factor, factor.T, precision=lax.Precision.HIGHEST) * hour_gram


def update(factor, totals, gram_part):
    return factor * totals / jnp.dot(gram_part, factor, precision=lax.Precision.HIGHEST)


def reference(counts, block_scales, anchor_factor, dest_factor, hour_factor):
    tensor = jnp.stack([dequantize(counts[hour_index], block_scales[hour_index]) for hour_index in range(HOURS)])
    hour_gram = jnp.dot(hour_factor.T, hour_factor, precision=lax.Precision.HIGHEST)
    anchor_now = anchor_factor
    dest_now = dest_factor
    for sweep_index in range(SWEEPS):
        dest_low = dest_now.astype(jnp.bfloat16)
        per_hour = jnp.einsum("rj,hij->hri", dest_low, tensor, preferred_element_type=jnp.float32)
        anchor_totals = jnp.einsum("hri,hr->ri", per_hour, hour_factor, precision=lax.Precision.HIGHEST)
        anchor_now = update(anchor_now, anchor_totals, gram_matrix(dest_now, hour_gram))
        anchor_low = anchor_now.astype(jnp.bfloat16)
        per_hour = jnp.einsum("ri,hij->hrj", anchor_low, tensor, preferred_element_type=jnp.float32)
        dest_totals = jnp.einsum("hrj,hr->rj", per_hour, hour_factor, precision=lax.Precision.HIGHEST)
        dest_now = update(dest_now, dest_totals, gram_matrix(anchor_now, hour_gram))
    return (anchor_now, dest_now)
```

```python
import jax
import jax.numpy as jnp
from jax import lax
from jax.experimental import pallas as pl
from jax.experimental.pallas import tpu as pltpu
from jax.sharding import PartitionSpec as P

RANK = 64
HOURS = 8
SWEEPS = 6
WIDE = 256
SLOTS = 4
MESH = pl.DeviceIdType.MESH
HIGHEST = lax.Precision.HIGHEST
F32 = jnp.float32
BF16 = jnp.bfloat16
FAR = (2, 1, 3, 0)
NEAR = (0, 1, 3, 2)
OFFSETS = sorted(
    [(dy, dx) for dy in range(4) for dx in range(4) if (dy, dx) != (0, 0)],
    key=lambda o: -(min(o[0], 4 - o[0]) + min(o[1], 4 - o[1])),
)


def flip(offset):
    return (4 - offset) % 4


def gram(left, right):
    return lax.dot_general(
        left, right, (((1,), (1,)), ((), ())), precision=HIGHEST, preferred_element_type=F32
    )


def kernel(
    counts_ref, scales_ref, anchor_ref, dest_ref, hour_ref,
    anchor_out, dest_out,
    tensor, tensor_t, stage, weights_a, weights_b, hours_wide, hour_gram,
    anchor_own, anchor_sib, dest, dest_own, sib_send, sib_recv, slabs,
    partial, partial_mine, parts, gram_send, gram_parts, kept,
    stage_sem, in_sem, sib_sems, half_sems, slab_send, slab_recv, part_send, part_recv,
    gsend, grecv, block_send, block_recv,
):
    o = lax.axis_index("org")
    d = lax.axis_index("dst")
    y, x = o // 4, lax.rem(o, 4)
    z, c = d // 2, lax.rem(d, 2)

    def org_peer(dy, dx):
        return (lax.rem(y + dy, 4) * 4 + lax.rem(x + dx, 4), d)

    def z_peer(dz):
        return (o, lax.rem(z + dz, 4) * 2 + c)

    sibling = (o, z * 2 + 1 - c)

    def rows16(index):
        return pl.ds(pl.multiple_of(index * 16, 16), 16)

    def rows8(index):
        return pl.ds(pl.multiple_of(index * 8, 8), 8)

    def stage_copy(step):
        hour, half = step // 2, lax.rem(step, 2)
        slot = lax.rem(step, SLOTS)
        return pltpu.make_async_copy(
            counts_ref.at[hour, pl.ds(pl.multiple_of(half * WIDE, WIDE), WIDE), :],
            stage.at[slot],
            stage_sem.at[slot],
        )

    for step in range(SLOTS):
        stage_copy(step).start()

    barrier = pltpu.get_barrier_semaphore()
    for dy, dx in OFFSETS:
        pl.semaphore_signal(barrier, inc=1, device_id=org_peer(dy, dx), device_id_type=MESH)
    for dz in (1, 2, 3):
        pl.semaphore_signal(barrier, inc=1, device_id=z_peer(dz), device_id_type=MESH)
    pl.semaphore_signal(barrier, inc=1, device_id=sibling, device_id_type=MESH)

    own_columns = pl.ds(pl.multiple_of(c * WIDE, WIDE), WIDE)
    first = [pltpu.make_async_copy(anchor_ref.at[:, own_columns], anchor_own, in_sem.at[0])]
    for chunk in range(4):
        first.append(
            pltpu.make_async_copy(
                dest_ref.at[:, pl.ds(chunk * WIDE, WIDE)], dest.at[chunk], in_sem.at[1 + chunk]
            )
        )
    for copy in first:
        copy.start()

    total = None
    for hour in range(HOURS):
        wide = jnp.broadcast_to(hour_ref[hour : hour + 1, :], (128, RANK)).T
        hours_wide[hour, :, 0:128] = wide
        hours_wide[hour, :, 128:256] = wide
        term = wide[:, 0:RANK] * hour_ref[hour : hour + 1, :]
        total = term if total is None else total + term
    hour_gram[...] = total

    def load(step, carry):
        hour, half = step // 2, lax.rem(step, 2)
        slot = lax.rem(step, SLOTS)
        stage_copy(step).wait()
        base = hour * WIDE
        for ib in range(2):
            for jb in range(8):
                scale = scales_ref[hour, half * 2 + ib, jb]
                block = stage[slot, ib * 128 : ib * 128 + 128, jb * 128 : jb * 128 + 128]
                values = (block.astype(F32) * scale).astype(BF16)
                row = pl.ds(pl.multiple_of(base + ib * 128, 128), 128)
                tensor[jb // 2, half, row, (jb % 2) * 128 : (jb % 2) * 128 + 128] = values
                row = pl.ds(pl.multiple_of(base + (jb % 2) * 128, 128), 128)
                tensor_t[half, jb // 2, row, ib * 128 : ib * 128 + 128] = values.T

        @pl.when(step + SLOTS < 2 * HOURS)
        def _():
            stage_copy(step + SLOTS).start()

        return carry

    lax.fori_loop(0, 2 * HOURS, load, 0)
    for copy in first:
        copy.wait()
    pl.semaphore_wait(barrier, 19)

    def spread(factor, weights):
        low = factor.astype(BF16).astype(F32)
        for hour in range(HOURS):
            scaled = low * hours_wide[hour]
            high = scaled.astype(BF16)
            rest = (scaled - high.astype(F32)).astype(BF16)
            weights[0:RANK, hour * WIDE : hour * WIDE + WIDE] = high
            weights[RANK : 2 * RANK, hour * WIDE : hour * WIDE + WIDE] = rest

    def fold(sums):
        return sums[0:RANK] + sums[RANK : 2 * RANK]

    def block_copy(dy, dx):
        where = dest.at[y, rows16(x)]
        return pltpu.make_async_remote_copy(
            where, where, block_send.at[dy * 4 + dx], block_recv.at[flip(dy) * 4 + flip(dx)],
            device_id=org_peer(dy, dx), device_id_type=MESH,
        )

    def block_arrival(dy, dx):
        where = dest.at[lax.rem(y + dy, 4), rows16(lax.rem(x + dx, 4))]
        return pltpu.make_async_remote_copy(
            where, where, block_send.at[dy * 4 + dx], block_recv.at[dy * 4 + dx],
            device_id=org_peer(dy, dx), device_id_type=MESH,
        )

    def part_copy(dy, dx):
        return pltpu.make_async_remote_copy(
            partial.at[dy, rows16(lax.rem(x + dx, 4))], parts.at[flip(dy) * 4 + flip(dx)],
            part_send.at[dy * 4 + dx], part_recv.at[flip(dy) * 4 + flip(dx)],
            device_id=org_peer(dy, dx), device_id_type=MESH,
        )

    def part_arrival(dy, dx):
        return pltpu.make_async_remote_copy(
            partial.at[dy, rows16(lax.rem(x + dx, 4))], parts.at[dy * 4 + dx],
            part_send.at[dy * 4 + dx], part_recv.at[dy * 4 + dx],
            device_id=org_peer(dy, dx), device_id_type=MESH,
        )

    def gram_copy(dy, dx):
        return pltpu.make_async_remote_copy(
            gram_send.at[rows8(lax.rem(x + dx, 4))], gram_parts.at[flip(dy) * 4 + flip(dx)],
            gsend.at[dy * 4 + dx], grecv.at[flip(dy) * 4 + flip(dx)],
            device_id=org_peer(dy, dx), device_id_type=MESH,
        )

    def gram_arrival(dy, dx):
        return pltpu.make_async_remote_copy(
            gram_send.at[rows8(lax.rem(x + dx, 4))], gram_parts.at[dy * 4 + dx],
            gsend.at[dy * 4 + dx], grecv.at[dy * 4 + dx],
            device_id=org_peer(dy, dx), device_id_type=MESH,
        )

    sib_copy = pltpu.make_async_remote_copy(
        sib_send, sib_recv, sib_sems.at[0], sib_sems.at[1], device_id=sibling, device_id_type=MESH
    )
    half_copy = pltpu.make_async_remote_copy(
        anchor_own, anchor_sib, half_sems.at[0], half_sems.at[1],
        device_id=sibling, device_id_type=MESH,
    )

    def sweep(index, carry):
        parity = lax.rem(index, 2)

        dest_gram = None
        for k, dy in enumerate(NEAR):
            chunk = lax.rem(y + dy, 4)

            @pl.when(index > 0)
            def _():
                for dx in NEAR:
                    if (dy, dx) != (0, 0):
                        block_arrival(dy, dx).wait_recv()

            values = dest[chunk]
            if dy == 0:
                dest_own[...] = values
            spread(values, weights_b)
            term = gram(values, values)
            dest_gram = term if dest_gram is None else dest_gram + term
            if k < 3:
                for half in range(2):
                    sums = jnp.dot(
                        weights_b[...], tensor_t[half, chunk], preferred_element_type=F32
                    )
                    if k == 0:
                        kept[half] = sums
                    else:
                        kept[half] += sums
            else:
                packed = jnp.concatenate(
                    [dest_gram[16 * q : 16 * q + 16] for q in range(4)], axis=1
                )
                sums = jnp.dot(
                    weights_b[...], tensor_t[1 - c, chunk], preferred_element_type=F32
                )
                sib_send[0:RANK] = fold(kept[1 - c] + sums)
                sib_send[RANK : RANK + 16] = packed
                sib_copy.start()
                sums = jnp.dot(weights_b[...], tensor_t[c, chunk], preferred_element_type=F32)
                mine = fold(kept[c] + sums)

        sib_copy.wait_recv()
        slabs[parity, z, 0:RANK] = mine + sib_recv[0:RANK]
        slabs[parity, z, RANK : RANK + 16] = packed + sib_recv[RANK : RANK + 16]

        def slab_copy(dz):
            return pltpu.make_async_remote_copy(
                slabs.at[parity, z], slabs.at[parity, z],
                slab_send.at[dz], slab_recv.at[parity, flip(dz)],
                device_id=z_peer(dz), device_id_type=MESH,
            )

        def slab_arrival(dz):
            where = slabs.at[parity, lax.rem(z + dz, 4)]
            return pltpu.make_async_remote_copy(
                where, where, slab_send.at[dz], slab_recv.at[parity, dz],
                device_id=z_peer(dz), device_id_type=MESH,
            )

        for dz in (2, 1, 3):
            slab_copy(dz).start()
        sib_copy.wait_send()
        for dz in (1, 3, 2):
            slab_arrival(dz).wait_recv()
        summed = slabs[parity, 0] + slabs[parity, 1] + slabs[parity, 2] + slabs[parity, 3]
        square = jnp.concatenate(
            [summed[RANK : RANK + 16, 64 * q : 64 * q + 64] for q in range(4)], axis=0
        )
        below = jnp.dot(
            square * hour_gram[...], anchor_own[...], precision=HIGHEST, preferred_element_type=F32
        )
        anchor_own[...] = anchor_own[...] * summed[0:RANK] / below
        half_copy.start()
        for dz in (1, 2, 3):
            slab_copy(dz).wait_send()

        mine = anchor_own[...]
        spread(mine, weights_a.at[0])
        anchor_gram = gram(mine, mine)
        for dy in FAR:
            kept[dy] = jnp.dot(
                weights_a[0], tensor[lax.rem(y + dy, 4), c], preferred_element_type=F32
            )
        half_copy.wait()
        other = anchor_sib[...]
        spread(other, weights_a.at[1])
        anchor_gram = anchor_gram + gram(other, other)
        for q in range(4):
            gram_send[8 * q : 8 * q + 8, 0:64] = anchor_gram[16 * q : 16 * q + 8]
            gram_send[8 * q : 8 * q + 8, 64:128] = anchor_gram[16 * q + 8 : 16 * q + 16]
        for dy, dx in OFFSETS:
            gram_copy(dy, dx).start()
        for dy in FAR:
            sums = kept[dy] + jnp.dot(
                weights_a[1], tensor[lax.rem(y + dy, 4), 1 - c], preferred_element_type=F32
            )
            partial[dy] = fold(sums)
            for dx in FAR:
                if (dy, dx) != (0, 0):
                    part_copy(dy, dx).start()

        square = gram_send[rows8(x)]
        for dy, dx in OFFSETS:
            gram_arrival(dy, dx).wait_recv()
            square = square + gram_parts[dy * 4 + dx]
        square = jnp.concatenate([square[:, 0:64], square[:, 64:128]], axis=0)
        below = jnp.dot(
            square * hour_gram[rows16(x)], dest_own[...],
            precision=HIGHEST, preferred_element_type=F32,
        )
        ratio = dest_own[rows16(x)] / below
        summed = partial[0, rows16(x)]
        for dy, dx in reversed(OFFSETS):
            part_arrival(dy, dx).wait_recv()
            summed = summed + parts[dy * 4 + dx]
        dest[y, rows16(x)] = ratio * summed
        for dy, dx in OFFSETS:
            block_copy(dy, dx).start()
        for dy, dx in OFFSETS:
            gram_copy(dy, dx).wait_send()
            part_copy(dy, dx).wait_send()
            block_copy(dy, dx).wait_send()
        return carry

    lax.fori_loop(0, SWEEPS, sweep, 0)

    anchor_out[:, own_columns] = anchor_own[...]
    anchor_out[:, pl.ds(pl.multiple_of((1 - c) * WIDE, WIDE), WIDE)] = anchor_sib[...]
    for dy, dx in reversed(OFFSETS):
        block_arrival(dy, dx).wait_recv()
    for chunk in range(4):
        dest_out[:, chunk * WIDE : chunk * WIDE + WIDE] = dest[chunk]


def body(counts, block_scales, anchor_factor, dest_factor, hour_factor):
    hbm = pl.BlockSpec(memory_space=pltpu.HBM)
    vmem = pl.BlockSpec(memory_space=pltpu.VMEM)
    dma = pltpu.SemaphoreType.DMA
    columns = dest_factor.shape[1]
    rows = anchor_factor.shape[1]
    return pl.pallas_call(
        kernel,
        out_shape=(
            jax.ShapeDtypeStruct((RANK, rows), F32),
            jax.ShapeDtypeStruct((RANK, columns), F32),
        ),
        in_specs=[hbm, pl.BlockSpec(memory_space=pltpu.SMEM), hbm, hbm, vmem],
        out_specs=(vmem, vmem),
        scratch_shapes=[
            pltpu.VMEM((4, 2, HOURS * WIDE, WIDE), BF16),
            pltpu.VMEM((2, 4, HOURS * WIDE, WIDE), BF16),
            pltpu.VMEM((SLOTS, WIDE, 4 * WIDE), jnp.int32),
            pltpu.VMEM((2, 2 * RANK, HOURS * WIDE), BF16),
            pltpu.VMEM((2 * RANK, HOURS * WIDE), BF16),
            pltpu.VMEM((HOURS, RANK, WIDE), F32),
            pltpu.VMEM((RANK, RANK), F32),
            pltpu.VMEM((RANK, WIDE), F32),
            pltpu.VMEM((RANK, WIDE), F32),
            pltpu.VMEM((4, RANK, WIDE), F32),
            pltpu.VMEM((RANK, WIDE), F32),
            pltpu.VMEM((RANK + 16, WIDE), F32),
            pltpu.VMEM((RANK + 16, WIDE), F32),
            pltpu.VMEM((2, 4, RANK + 16, WIDE), F32),
            pltpu.VMEM((4, RANK, WIDE), F32),
            pltpu.VMEM((8, 128), F32),
            pltpu.VMEM((16, 16, WIDE), F32),
            pltpu.VMEM((32, 128), F32),
            pltpu.VMEM((16, 8, 128), F32),
            pltpu.VMEM((4, 2 * RANK, WIDE), F32),
            dma((SLOTS,)),
            dma((5,)),
            dma((2,)),
            dma((2,)),
            dma((4,)),
            dma((2, 4)),
            dma((16,)),
            dma((16,)),
            dma((16,)),
            dma((16,)),
            dma((16,)),
            dma((16,)),
        ],
        compiler_params=pltpu.CompilerParams(
            collective_id=0, has_side_effects=True, vmem_limit_bytes=48 * 1024 * 1024
        ),
        name="sweeps",
    )(counts, block_scales, anchor_factor, dest_factor, hour_factor)


def solution(mesh):
    return jax.shard_map(
        body,
        mesh=mesh,
        in_specs=(
            P(None, "org", "dst"),
            P(None, "org", "dst"),
            P(None, "org"),
            P(None, "dst"),
            P(),
        ),
        out_specs=(P(None, "org"), P(None, "dst")),
        check_vma=False,
    )
```

```python
import jax
import jax.numpy as jnp
from jax import lax
from jax.experimental import pallas as pl
from jax.experimental.pallas import tpu as pltpu
from jax.sharding import PartitionSpec as P

RANK = 64
HOURS = 8
SWEEPS = 6
WIDE = 256
SLOTS = 4
MESH = pl.DeviceIdType.MESH
HIGHEST = lax.Precision.HIGHEST
F32 = jnp.float32
BF16 = jnp.bfloat16
FAR = (2, 1, 3, 0)
NEAR = (0, 1, 3, 2)
OFFSETS = sorted(
    [(dy, dx) for dy in range(4) for dx in range(4) if (dy, dx) != (0, 0)],
    key=lambda o: -(min(o[0], 4 - o[0]) + min(o[1], 4 - o[1])),
)


def flip(offset):
    return (4 - offset) % 4


def gram(left, right):
    return lax.dot_general(
        left, right, (((1,), (1,)), ((), ())), precision=HIGHEST, preferred_element_type=F32
    )


def kernel(
    counts_ref, scales_ref, anchor_ref, dest_ref, hour_ref,
    anchor_out, dest_out,
    tensor, tensor_t, stage, scales, hours, weights_a, weights_b, hours_wide, hour_gram,
    anchor_own, anchor_sib, dest, dest_own, mine, sib_send, sib_recv, sib_gram, sib_gram_recv,
    org_gram, org_gram_recv,
    slabs, gram_slabs, partial, parts, gram_send, gram_parts, kept, square_sum,
    stage_sem, in_sem, sib_sems, half_sems, slab_send, slab_recv, gslab_send, gslab_recv,
    part_send, part_recv, gsend, grecv, block_send, block_recv,
):
    o = lax.axis_index("org")
    d = lax.axis_index("dst")
    y, x = o // 4, lax.rem(o, 4)
    z, c = d // 2, lax.rem(d, 2)

    def org_peer(dy, dx):
        return (lax.rem(y + dy, 4) * 4 + lax.rem(x + dx, 4), d)

    def z_peer(dz):
        return (o, lax.rem(z + dz, 4) * 2 + c)

    sibling = (o, z * 2 + 1 - c)

    def rows16(index):
        return pl.ds(pl.multiple_of(index * 16, 16), 16)

    def rows8(index):
        return pl.ds(pl.multiple_of(index * 8, 8), 8)

    def rows_of(hour):
        return pl.ds(pl.multiple_of(hour * WIDE, WIDE), WIDE)

    def stage_copy(step):
        hour, half = lax.rem(step, 8), lax.rem(1 - c + step // 8, 2)
        slot = lax.rem(step, SLOTS)
        return pltpu.make_async_copy(
            counts_ref.at[hour, rows_of(half), :], stage.at[slot], stage_sem.at[slot]
        )

    own_columns = rows_of(c)
    first = [
        pltpu.make_async_copy(scales_ref, scales, in_sem.at[0]),
        pltpu.make_async_copy(hour_ref, hours, in_sem.at[1]),
        pltpu.make_async_copy(anchor_ref.at[:, own_columns], anchor_own, in_sem.at[2]),
    ]
    for chunk in range(4):
        first.append(
            pltpu.make_async_copy(
                dest_ref.at[:, pl.ds(chunk * WIDE, WIDE)], dest.at[chunk], in_sem.at[3 + chunk]
            )
        )
    for copy in first:
        copy.start()
    for step in range(SLOTS):
        stage_copy(step).start()

    barrier = pltpu.get_barrier_semaphore()
    for dy, dx in OFFSETS:
        pl.semaphore_signal(barrier, inc=1, device_id=org_peer(dy, dx), device_id_type=MESH)
    for dz in (1, 2, 3):
        pl.semaphore_signal(barrier, inc=1, device_id=z_peer(dz), device_id_type=MESH)
    pl.semaphore_signal(barrier, inc=1, device_id=sibling, device_id_type=MESH)

    for copy in first:
        copy.wait()

    total = None
    for hour in range(HOURS):
        wide = jnp.broadcast_to(hours[hour : hour + 1, :], (128, RANK)).T
        hours_wide[hour, :, 0:128] = wide
        hours_wide[hour, :, 128:256] = wide
        term = wide[:, 0:RANK] * hours[hour : hour + 1, :]
        total = term if total is None else total + term
    hour_gram[...] = total

    def spread(factor, weights):
        low = factor.astype(BF16).astype(F32)
        for hour in range(HOURS):
            scaled = low * hours_wide[hour]
            high = scaled.astype(BF16)
            rest = (scaled - high.astype(F32)).astype(BF16)
            weights[0:RANK, hour * WIDE : hour * WIDE + WIDE] = high
            weights[RANK : 2 * RANK, hour * WIDE : hour * WIDE + WIDE] = rest

    def fold(sums):
        return sums[0:RANK] + sums[RANK : 2 * RANK]

    def pack(square):
        return jnp.concatenate([square[16 * q : 16 * q + 16] for q in range(4)], axis=1)

    dest_gram = None
    for chunk in range(4):
        spread(dest[chunk], weights_b.at[chunk])
        term = gram(dest[chunk], dest[chunk])
        dest_gram = term if dest_gram is None else dest_gram + term
    dest_own[...] = dest[y]
    gram_slabs[0, z] = pack(dest_gram)
    kept[...] = jnp.zeros_like(kept)

    sib_copy = pltpu.make_async_remote_copy(
        sib_send, sib_recv, sib_sems.at[0], sib_sems.at[1], device_id=sibling, device_id_type=MESH
    )
    sib_gram_copy = pltpu.make_async_remote_copy(
        sib_gram, sib_gram_recv, sib_sems.at[2], sib_sems.at[3],
        device_id=sibling, device_id_type=MESH,
    )
    org_gram_copy = pltpu.make_async_remote_copy(
        org_gram, org_gram_recv, sib_sems.at[4], sib_sems.at[5],
        device_id=sibling, device_id_type=MESH,
    )
    half_copy = pltpu.make_async_remote_copy(
        anchor_own, anchor_sib, half_sems.at[0], half_sems.at[1],
        device_id=sibling, device_id_type=MESH,
    )

    def z_copy(slots, send, recv, parity, dz):
        return pltpu.make_async_remote_copy(
            slots.at[parity, z], slots.at[parity, z], send.at[dz], recv.at[parity, flip(dz)],
            device_id=z_peer(dz), device_id_type=MESH,
        )

    def z_arrival(slots, send, recv, parity, dz):
        where = slots.at[parity, lax.rem(z + dz, 4)]
        return pltpu.make_async_remote_copy(
            where, where, send.at[dz], recv.at[parity, dz],
            device_id=z_peer(dz), device_id_type=MESH,
        )

    slab = (slabs, slab_send, slab_recv)
    gram_slab = (gram_slabs, gslab_send, gslab_recv)

    def load(step, carry):
        hour, half = lax.rem(step, 8), lax.rem(1 - c + step // 8, 2)
        slot = lax.rem(step, SLOTS)
        stage_copy(step).wait()
        for ib in range(2):
            for jb in range(8):
                scale = scales[hour, half * 2 + ib, jb]
                block = stage[slot, ib * 128 : ib * 128 + 128, jb * 128 : jb * 128 + 128]
                values = (block.astype(F32) * scale).astype(BF16)
                row = pl.ds(pl.multiple_of(hour * WIDE + ib * 128, 128), 128)
                tensor[jb // 2, half, row, (jb % 2) * 128 : (jb % 2) * 128 + 128] = values

        @pl.when(step + SLOTS < 2 * HOURS)
        def _():
            stage_copy(step + SLOTS).start()

        sums = kept[step // 8]
        for chunk in range(4):
            sums = sums + lax.dot_general(
                weights_b[chunk, :, rows_of(hour)], tensor[chunk, half, rows_of(hour), :],
                (((1,), (1,)), ((), ())), preferred_element_type=F32,
            )
        kept[step // 8] = sums
        return carry

    lax.fori_loop(0, HOURS, load, 0)
    sib_send[...] = fold(kept[0])
    pl.semaphore_wait(barrier, 19)
    sib_copy.start()
    for dz in (2, 1, 3):
        z_copy(*gram_slab, 0, dz).start()
    lax.fori_loop(HOURS, 2 * HOURS, load, 0)
    mine[...] = fold(kept[1])

    def block_copy(dy, dx):
        where = dest.at[y, rows16(x)]
        return pltpu.make_async_remote_copy(
            where, where, block_send.at[dy * 4 + dx], block_recv.at[flip(dy) * 4 + flip(dx)],
            device_id=org_peer(dy, dx), device_id_type=MESH,
        )

    def block_arrival(dy, dx):
        where = dest.at[lax.rem(y + dy, 4), rows16(lax.rem(x + dx, 4))]
        return pltpu.make_async_remote_copy(
            where, where, block_send.at[dy * 4 + dx], block_recv.at[dy * 4 + dx],
            device_id=org_peer(dy, dx), device_id_type=MESH,
        )

    def part_copy(dy, dx):
        return pltpu.make_async_remote_copy(
            partial.at[dy, rows16(lax.rem(x + dx, 4))], parts.at[flip(dy) * 4 + flip(dx)],
            part_send.at[dy * 4 + dx], part_recv.at[flip(dy) * 4 + flip(dx)],
            device_id=org_peer(dy, dx), device_id_type=MESH,
        )

    def part_arrival(dy, dx):
        return pltpu.make_async_remote_copy(
            partial.at[dy, rows16(lax.rem(x + dx, 4))], parts.at[dy * 4 + dx],
            part_send.at[dy * 4 + dx], part_recv.at[dy * 4 + dx],
            device_id=org_peer(dy, dx), device_id_type=MESH,
        )

    def gram_copy(dy, dx):
        return pltpu.make_async_remote_copy(
            gram_send.at[rows8(lax.rem(x + dx, 4))], gram_parts.at[flip(dy) * 4 + flip(dx)],
            gsend.at[dy * 4 + dx], grecv.at[flip(dy) * 4 + flip(dx)],
            device_id=org_peer(dy, dx), device_id_type=MESH,
        )

    def gram_arrival(dy, dx):
        return pltpu.make_async_remote_copy(
            gram_send.at[rows8(lax.rem(x + dx, 4))], gram_parts.at[dy * 4 + dx],
            gsend.at[dy * 4 + dx], grecv.at[dy * 4 + dx],
            device_id=org_peer(dy, dx), device_id_type=MESH,
        )

    def sweep(index, carry):
        parity = lax.rem(index, 2)

        sib_copy.wait_recv()
        slabs[parity, z] = mine[...] + sib_recv[...]
        for dz in (2, 1, 3):
            z_copy(*slab, parity, dz).start()
        sib_copy.wait_send()

        @pl.when(index == 0)
        def _():
            def turn(step, carry):
                half, chunk = lax.rem(step, 2), lax.rem(step // 2, 4)
                hour = rows_of(step // 8)
                tensor_t[half, chunk, hour, :] = tensor[chunk, half, hour, :].T
                return carry

            lax.fori_loop(0, 8 * HOURS, turn, 0)

        for dz in (1, 3, 2):
            z_arrival(*gram_slab, parity, dz).wait_recv()
        summed = (gram_slabs[parity, 0] + gram_slabs[parity, 1]) + (
            gram_slabs[parity, 2] + gram_slabs[parity, 3]
        )
        sib_gram[...] = summed
        sib_gram_copy.start()
        for dz in (1, 2, 3):
            z_copy(*gram_slab, parity, dz).wait_send()
        sib_gram_copy.wait()
        summed = summed + sib_gram_recv[...]
        square = jnp.concatenate([summed[:, 64 * q : 64 * q + 64] for q in range(4)], axis=0)
        below = jnp.dot(
            square * hour_gram[...], anchor_own[...], precision=HIGHEST, preferred_element_type=F32
        )
        ratio = anchor_own[...] / below
        for dz in (1, 3, 2):
            z_arrival(*slab, parity, dz).wait_recv()
        summed = (slabs[parity, 0] + slabs[parity, 1]) + (slabs[parity, 2] + slabs[parity, 3])
        own = ratio * summed
        anchor_own[...] = own
        half_copy.start()

        spread(own, weights_a.at[0])
        anchor_gram = gram(own, own)
        for q in range(4):
            low, high = 8 * q, 8 * q + 8
            gram_send[low:high, 0:64] = anchor_gram[16 * q : 16 * q + 8]
            gram_send[low:high, 64:128] = anchor_gram[16 * q + 8 : 16 * q + 16]
        for dy, dx in OFFSETS:
            gram_copy(dy, dx).start()
        for dy in FAR:
            kept[dy] = jnp.dot(
                weights_a[0], tensor[lax.rem(y + dy, 4), c], preferred_element_type=F32
            )
        for dz in (1, 2, 3):
            z_copy(*slab, parity, dz).wait_send()
        half_copy.wait()
        other = anchor_sib[...]
        spread(other, weights_a.at[1])
        for dy in FAR:
            sums = kept[dy] + jnp.dot(
                weights_a[1], tensor[lax.rem(y + dy, 4), 1 - c], preferred_element_type=F32
            )
            partial[dy] = fold(sums)
            for dx in FAR:
                if (dy, dx) != (0, 0):
                    part_copy(dy, dx).start()

        square = gram_send[rows8(x)]
        for dy, dx in reversed(OFFSETS):
            gram_arrival(dy, dx).wait_recv()
            square = square + gram_parts[dy * 4 + dx]
        org_gram[...] = square
        org_gram_copy.start()
        org_gram_copy.wait()
        square = square + org_gram_recv[...]
        square = jnp.concatenate([square[:, 0:64], square[:, 64:128]], axis=0)
        below = jnp.dot(
            square * hour_gram[rows16(x)], dest_own[...],
            precision=HIGHEST, preferred_element_type=F32,
        )
        ratio = dest_own[rows16(x)] / below
        summed = partial[0, rows16(x)]
        for dy, dx in reversed(OFFSETS):
            part_arrival(dy, dx).wait_recv()
            summed = summed + parts[dy * 4 + dx]
        dest[y, rows16(x)] = ratio * summed
        for dy, dx in OFFSETS:
            block_copy(dy, dx).start()
        for dy, dx in OFFSETS:
            gram_copy(dy, dx).wait_send()
            part_copy(dy, dx).wait_send()

        for k, dy in enumerate(NEAR):
            chunk = lax.rem(y + dy, 4)
            for dx in NEAR:
                if (dy, dx) != (0, 0):
                    block_arrival(dy, dx).wait_recv()

            @pl.when(index < SWEEPS - 1)
            def _():
                values = dest[chunk]
                weights = weights_b.at[k]
                spread(values, weights)
                if dy == 0:
                    dest_own[...] = values
                if k < 3:
                    for half in range(2):
                        sums = jnp.dot(
                            weights[...], tensor_t[half, chunk], preferred_element_type=F32
                        )
                        if k == 0:
                            kept[half] = sums
                        else:
                            kept[half] += sums
                    term = gram(values, values)
                    if k == 0:
                        square_sum[...] = term
                    else:
                        square_sum[...] += term
                else:
                    sums = jnp.dot(
                        weights[...], tensor_t[1 - c, chunk], preferred_element_type=F32
                    )
                    sib_send[...] = fold(kept[1 - c] + sums)
                    sib_copy.start()
                    gram_slabs[1 - parity, z] = pack(square_sum[...] + gram(values, values))
                    for dz in (2, 1, 3):
                        z_copy(*gram_slab, 1 - parity, dz).start()
                    sums = jnp.dot(weights[...], tensor_t[c, chunk], preferred_element_type=F32)
                    mine[...] = fold(kept[c] + sums)

        for dy, dx in OFFSETS:
            block_copy(dy, dx).wait_send()
        return carry

    lax.fori_loop(0, SWEEPS, sweep, 0)

    anchor_out[:, own_columns] = anchor_own[...]
    anchor_out[:, rows_of(1 - c)] = anchor_sib[...]
    for chunk in range(4):
        dest_out[:, chunk * WIDE : chunk * WIDE + WIDE] = dest[chunk]


def body(counts, block_scales, anchor_factor, dest_factor, hour_factor):
    hbm = pl.BlockSpec(memory_space=pltpu.HBM)
    vmem = pl.BlockSpec(memory_space=pltpu.VMEM)
    dma = pltpu.SemaphoreType.DMA
    columns = dest_factor.shape[1]
    rows = anchor_factor.shape[1]
    small = [
        pltpu.with_memory_space_constraint(value, pltpu.HBM)
        for value in (block_scales, anchor_factor, dest_factor, hour_factor)
    ]
    return pl.pallas_call(
        kernel,
        out_shape=(
            jax.ShapeDtypeStruct((RANK, rows), F32),
            jax.ShapeDtypeStruct((RANK, columns), F32),
        ),
        in_specs=[hbm] * 5,
        out_specs=(vmem, vmem),
        scratch_shapes=[
            pltpu.VMEM((4, 2, HOURS * WIDE, WIDE), BF16),
            pltpu.VMEM((2, 4, HOURS * WIDE, WIDE), BF16),
            pltpu.VMEM((SLOTS, WIDE, 4 * WIDE), jnp.int32),
            pltpu.SMEM((HOURS, 4, 8), F32),
            pltpu.VMEM((HOURS, RANK), F32),
            pltpu.VMEM((2, 2 * RANK, HOURS * WIDE), BF16),
            pltpu.VMEM((4, 2 * RANK, HOURS * WIDE), BF16),
            pltpu.VMEM((HOURS, RANK, WIDE), F32),
            pltpu.VMEM((RANK, RANK), F32),
            pltpu.VMEM((RANK, WIDE), F32),
            pltpu.VMEM((RANK, WIDE), F32),
            pltpu.VMEM((4, RANK, WIDE), F32),
            pltpu.VMEM((RANK, WIDE), F32),
            pltpu.VMEM((RANK, WIDE), F32),
            pltpu.VMEM((RANK, WIDE), F32),
            pltpu.VMEM((RANK, WIDE), F32),
            pltpu.VMEM((16, WIDE), F32),
            pltpu.VMEM((16, WIDE), F32),
            pltpu.VMEM((8, 128), F32),
            pltpu.VMEM((8, 128), F32),
            pltpu.VMEM((2, 4, RANK, WIDE), F32),
            pltpu.VMEM((2, 4, 16, WIDE), F32),
            pltpu.VMEM((4, RANK, WIDE), F32),
            pltpu.VMEM((16, 16, WIDE), F32),
            pltpu.VMEM((32, 128), F32),
            pltpu.VMEM((16, 8, 128), F32),
            pltpu.VMEM((4, 2 * RANK, WIDE), F32),
            pltpu.VMEM((RANK, RANK), F32),
            dma((SLOTS,)),
            dma((7,)),
            dma((6,)),
            dma((2,)),
            dma((4,)),
            dma((2, 4)),
            dma((4,)),
            dma((2, 4)),
            dma((16,)),
            dma((16,)),
            dma((16,)),
            dma((16,)),
            dma((16,)),
            dma((16,)),
        ],
        compiler_params=pltpu.CompilerParams(
            collective_id=0, has_side_effects=True, vmem_limit_bytes=50 * 1024 * 1024
        ),
        name="sweeps",
    )(counts, *small)


def solution(mesh):
    return jax.shard_map(
        body,
        mesh=mesh,
        in_specs=(
            P(None, "org", "dst"),
            P(None, "org", "dst"),
            P(None, "org"),
            P(None, "dst"),
            P(),
        ),
        out_specs=(P(None, "org"), P(None, "dst")),
        check_vma=False,
    )
```

```python
import jax
import jax.numpy as jnp
from jax import lax
from jax.experimental import pallas as pl
from jax.experimental.pallas import tpu as pltpu
from jax.sharding import PartitionSpec as P

RANK = 64
HOURS = 8
SWEEPS = 6
WIDE = 256
SLOTS = 4
MESH = pl.DeviceIdType.MESH
HIGHEST = lax.Precision.HIGHEST
F32 = jnp.float32
BF16 = jnp.bfloat16
FAR = (2, 1, 3, 0)
NEAR = (0, 1, 3, 2)
OFFSETS = sorted(
    [(dy, dx) for dy in range(4) for dx in range(4) if (dy, dx) != (0, 0)],
    key=lambda o: -(min(o[0], 4 - o[0]) + min(o[1], 4 - o[1])),
)


def flip(offset):
    return (4 - offset) % 4


def gram(left, right):
    return lax.dot_general(
        left, right, (((1,), (1,)), ((), ())), precision=HIGHEST, preferred_element_type=F32
    )


def kernel(
    counts_ref, scales_ref, anchor_ref, dest_ref, hour_ref,
    anchor_out, dest_out,
    tensor, tensor_t, stage, scales, hours, weights_a, weights_b, hours_wide, hour_gram,
    anchor_own, anchor_sib, dest, dest_own, mine, sib_send, sib_recv, sib_gram, sib_gram_recv,
    org_gram, org_gram_recv,
    slabs, gram_slabs, partial, parts, gram_send, gram_parts, kept, square_sum,
    stage_sem, in_sem, sib_sems, half_sems, slab_send, slab_recv, gslab_send, gslab_recv,
    part_send, part_recv, gsend, grecv, block_send, block_recv,
):
    o = lax.axis_index("org")
    d = lax.axis_index("dst")
    y, x = o // 4, lax.rem(o, 4)
    z, c = d // 2, lax.rem(d, 2)

    def org_peer(dy, dx):
        return (lax.rem(y + dy, 4) * 4 + lax.rem(x + dx, 4), d)

    def z_peer(dz):
        return (o, lax.rem(z + dz, 4) * 2 + c)

    sibling = (o, z * 2 + 1 - c)

    def rows16(index):
        return pl.ds(pl.multiple_of(index * 16, 16), 16)

    def rows8(index):
        return pl.ds(pl.multiple_of(index * 8, 8), 8)

    def rows_of(hour):
        return pl.ds(pl.multiple_of(hour * WIDE, WIDE), WIDE)

    def stage_copy(step):
        hour, half = lax.rem(step, 8), lax.rem(1 - c + step // 8, 2)
        slot = lax.rem(step, SLOTS)
        return pltpu.make_async_copy(
            counts_ref.at[hour, rows_of(half), :], stage.at[slot], stage_sem.at[slot]
        )

    own_columns = rows_of(c)
    first = [
        pltpu.make_async_copy(scales_ref, scales, in_sem.at[0]),
        pltpu.make_async_copy(hour_ref, hours, in_sem.at[1]),
        pltpu.make_async_copy(anchor_ref.at[:, own_columns], anchor_own, in_sem.at[2]),
    ]
    for chunk in range(4):
        first.append(
            pltpu.make_async_copy(
                dest_ref.at[:, pl.ds(chunk * WIDE, WIDE)], dest.at[chunk], in_sem.at[3 + chunk]
            )
        )
    for copy in first:
        copy.start()
    for step in range(SLOTS):
        stage_copy(step).start()

    barrier = pltpu.get_barrier_semaphore()
    for dy, dx in OFFSETS:
        pl.semaphore_signal(barrier, inc=1, device_id=org_peer(dy, dx), device_id_type=MESH)
    for dz in (1, 2, 3):
        pl.semaphore_signal(barrier, inc=1, device_id=z_peer(dz), device_id_type=MESH)
    pl.semaphore_signal(barrier, inc=1, device_id=sibling, device_id_type=MESH)

    for copy in first:
        copy.wait()

    total = None
    for hour in range(HOURS):
        wide = jnp.broadcast_to(hours[hour : hour + 1, :], (128, RANK)).T
        hours_wide[hour, :, 0:128] = wide
        hours_wide[hour, :, 128:256] = wide
        term = wide[:, 0:RANK] * hours[hour : hour + 1, :]
        total = term if total is None else total + term
    hour_gram[...] = total

    def spread(factor, weights):
        low = factor.astype(BF16).astype(F32)
        for hour in range(HOURS):
            scaled = low * hours_wide[hour]
            high = scaled.astype(BF16)
            rest = (scaled - high.astype(F32)).astype(BF16)
            weights[0:RANK, hour * WIDE : hour * WIDE + WIDE] = high
            weights[RANK : 2 * RANK, hour * WIDE : hour * WIDE + WIDE] = rest

    def fold(sums):
        return sums[0:RANK] + sums[RANK : 2 * RANK]

    def pack(square):
        return jnp.concatenate([square[16 * q : 16 * q + 16] for q in range(4)], axis=1)

    dest_gram = None
    for chunk in range(4):
        spread(dest[chunk], weights_b.at[chunk])
        term = gram(dest[chunk], dest[chunk])
        dest_gram = term if dest_gram is None else dest_gram + term
    dest_own[...] = dest[y]
    gram_slabs[0, z] = pack(dest_gram)
    kept[...] = jnp.zeros_like(kept)

    sib_copy = pltpu.make_async_remote_copy(
        sib_send, sib_recv, sib_sems.at[0], sib_sems.at[1], device_id=sibling, device_id_type=MESH
    )
    sib_gram_copy = pltpu.make_async_remote_copy(
        sib_gram, sib_gram_recv, sib_sems.at[2], sib_sems.at[3],
        device_id=sibling, device_id_type=MESH,
    )
    org_gram_copy = pltpu.make_async_remote_copy(
        org_gram, org_gram_recv, sib_sems.at[4], sib_sems.at[5],
        device_id=sibling, device_id_type=MESH,
    )
    half_copy = pltpu.make_async_remote_copy(
        anchor_own, anchor_sib, half_sems.at[0], half_sems.at[1],
        device_id=sibling, device_id_type=MESH,
    )

    def z_copy(slots, send, recv, parity, dz):
        return pltpu.make_async_remote_copy(
            slots.at[parity, z], slots.at[parity, z], send.at[dz], recv.at[parity, flip(dz)],
            device_id=z_peer(dz), device_id_type=MESH,
        )

    def z_arrival(slots, send, recv, parity, dz):
        where = slots.at[parity, lax.rem(z + dz, 4)]
        return pltpu.make_async_remote_copy(
            where, where, send.at[dz], recv.at[parity, dz],
            device_id=z_peer(dz), device_id_type=MESH,
        )

    slab = (slabs, slab_send, slab_recv)
    gram_slab = (gram_slabs, gslab_send, gslab_recv)

    def load(step, carry):
        hour, half = lax.rem(step, 8), lax.rem(1 - c + step // 8, 2)
        slot = lax.rem(step, SLOTS)
        stage_copy(step).wait()
        for ib in range(2):
            for jb in range(8):
                scale = scales[hour, half * 2 + ib, jb]
                block = stage[slot, ib * 128 : ib * 128 + 128, jb * 128 : jb * 128 + 128]
                values = (block.astype(F32) * scale).astype(BF16)
                row = pl.ds(pl.multiple_of(hour * WIDE + ib * 128, 128), 128)
                tensor[jb // 2, half, row, (jb % 2) * 128 : (jb % 2) * 128 + 128] = values

        @pl.when(step + SLOTS < 2 * HOURS)
        def _():
            stage_copy(step + SLOTS).start()

        sums = kept[step // 8]
        for chunk in range(4):
            sums = sums + lax.dot_general(
                weights_b[chunk, :, rows_of(hour)], tensor[chunk, half, rows_of(hour), :],
                (((1,), (1,)), ((), ())), preferred_element_type=F32,
            )
        kept[step // 8] = sums
        return carry

    lax.fori_loop(0, HOURS, load, 0)
    sib_send[...] = fold(kept[0])
    pl.semaphore_wait(barrier, 19)
    sib_copy.start()
    for dz in (2, 1, 3):
        z_copy(*gram_slab, 0, dz).start()
    lax.fori_loop(HOURS, 2 * HOURS, load, 0)
    mine[...] = fold(kept[1])

    def block_copy(dy, dx):
        where = dest.at[y, rows16(x)]
        return pltpu.make_async_remote_copy(
            where, where, block_send.at[dy * 4 + dx], block_recv.at[flip(dy) * 4 + flip(dx)],
            device_id=org_peer(dy, dx), device_id_type=MESH,
        )

    def block_arrival(dy, dx):
        where = dest.at[lax.rem(y + dy, 4), rows16(lax.rem(x + dx, 4))]
        return pltpu.make_async_remote_copy(
            where, where, block_send.at[dy * 4 + dx], block_recv.at[dy * 4 + dx],
            device_id=org_peer(dy, dx), device_id_type=MESH,
        )

    def part_copy(dy, dx):
        return pltpu.make_async_remote_copy(
            partial.at[dy, rows16(lax.rem(x + dx, 4))], parts.at[flip(dy) * 4 + flip(dx)],
            part_send.at[dy * 4 + dx], part_recv.at[flip(dy) * 4 + flip(dx)],
            device_id=org_peer(dy, dx), device_id_type=MESH,
        )

    def part_arrival(dy, dx):
        return pltpu.make_async_remote_copy(
            partial.at[dy, rows16(lax.rem(x + dx, 4))], parts.at[dy * 4 + dx],
            part_send.at[dy * 4 + dx], part_recv.at[dy * 4 + dx],
            device_id=org_peer(dy, dx), device_id_type=MESH,
        )

    def gram_copy(dy, dx):
        return pltpu.make_async_remote_copy(
            gram_send.at[rows8(lax.rem(x + dx, 4))], gram_parts.at[flip(dy) * 4 + flip(dx)],
            gsend.at[dy * 4 + dx], grecv.at[flip(dy) * 4 + flip(dx)],
            device_id=org_peer(dy, dx), device_id_type=MESH,
        )

    def gram_arrival(dy, dx):
        return pltpu.make_async_remote_copy(
            gram_send.at[rows8(lax.rem(x + dx, 4))], gram_parts.at[dy * 4 + dx],
            gsend.at[dy * 4 + dx], grecv.at[dy * 4 + dx],
            device_id=org_peer(dy, dx), device_id_type=MESH,
        )

    def turn(step, carry):
        half, chunk = lax.rem(step, 2), lax.rem(step // 2, 4)
        hour = rows_of(step // 8)
        tensor_t[half, chunk, hour, :] = tensor[chunk, half, hour, :].T
        return carry

    def sweep(index, carry):
        parity = lax.rem(index, 2)

        sib_copy.wait_recv()
        slabs[parity, z] = mine[...] + sib_recv[...]
        for dz in (2, 1, 3):
            z_copy(*slab, parity, dz).start()
        sib_copy.wait_send()

        @pl.when(index == 0)
        def _():
            lax.fori_loop(0, 4 * HOURS, turn, 0)

        for dz in (1, 3, 2):
            z_arrival(*gram_slab, parity, dz).wait_recv()
        summed = (gram_slabs[parity, 0] + gram_slabs[parity, 1]) + (
            gram_slabs[parity, 2] + gram_slabs[parity, 3]
        )
        sib_gram[...] = summed
        sib_gram_copy.start()
        for dz in (1, 2, 3):
            z_copy(*gram_slab, parity, dz).wait_send()
        sib_gram_copy.wait()
        summed = summed + sib_gram_recv[...]
        square = jnp.concatenate([summed[:, 64 * q : 64 * q + 64] for q in range(4)], axis=0)
        below = jnp.dot(
            square * hour_gram[...], anchor_own[...], precision=HIGHEST, preferred_element_type=F32
        )
        ratio = anchor_own[...] / below
        for dz in (1, 3, 2):
            z_arrival(*slab, parity, dz).wait_recv()
        summed = (slabs[parity, 0] + slabs[parity, 1]) + (slabs[parity, 2] + slabs[parity, 3])
        own = ratio * summed
        anchor_own[...] = own
        half_copy.start()

        spread(own, weights_a.at[0])
        anchor_gram = gram(own, own)
        for q in range(4):
            low, high = 8 * q, 8 * q + 8
            gram_send[low:high, 0:64] = anchor_gram[16 * q : 16 * q + 8]
            gram_send[low:high, 64:128] = anchor_gram[16 * q + 8 : 16 * q + 16]
        for dy, dx in OFFSETS:
            gram_copy(dy, dx).start()
        for dy in FAR:
            kept[dy] = jnp.dot(
                weights_a[0], tensor[lax.rem(y + dy, 4), c], preferred_element_type=F32
            )
        for dz in (1, 2, 3):
            z_copy(*slab, parity, dz).wait_send()
        half_copy.wait()
        other = anchor_sib[...]
        spread(other, weights_a.at[1])
        for dy in FAR:
            sums = kept[dy] + jnp.dot(
                weights_a[1], tensor[lax.rem(y + dy, 4), 1 - c], preferred_element_type=F32
            )
            partial[dy] = fold(sums)
            for dx in FAR:
                if (dy, dx) != (0, 0):
                    part_copy(dy, dx).start()

        @pl.when(index == 0)
        def _():
            lax.fori_loop(4 * HOURS, 8 * HOURS, turn, 0)

        square = gram_send[rows8(x)]
        for dy, dx in reversed(OFFSETS):
            gram_arrival(dy, dx).wait_recv()
            square = square + gram_parts[dy * 4 + dx]
        org_gram[...] = square
        org_gram_copy.start()
        org_gram_copy.wait()
        square = square + org_gram_recv[...]
        square = jnp.concatenate([square[:, 0:64], square[:, 64:128]], axis=0)
        below = jnp.dot(
            square * hour_gram[rows16(x)], dest_own[...],
            precision=HIGHEST, preferred_element_type=F32,
        )
        ratio = dest_own[rows16(x)] / below
        summed = partial[0, rows16(x)]
        for dy, dx in reversed(OFFSETS):
            part_arrival(dy, dx).wait_recv()
            summed = summed + parts[dy * 4 + dx]
        dest[y, rows16(x)] = ratio * summed
        for dy, dx in OFFSETS:
            block_copy(dy, dx).start()
        for dy, dx in OFFSETS:
            gram_copy(dy, dx).wait_send()
            part_copy(dy, dx).wait_send()

        for k, dy in enumerate(NEAR):
            chunk = lax.rem(y + dy, 4)
            for dx in NEAR:
                if (dy, dx) != (0, 0):
                    block_arrival(dy, dx).wait_recv()

            @pl.when(index < SWEEPS - 1)
            def _():
                values = dest[chunk]
                weights = weights_b.at[k]
                spread(values, weights)
                if dy == 0:
                    dest_own[...] = values
                if k < 3:
                    for half in range(2):
                        sums = jnp.dot(
                            weights[...], tensor_t[half, chunk], preferred_element_type=F32
                        )
                        if k == 0:
                            kept[half] = sums
                        else:
                            kept[half] += sums
                    term = gram(values, values)
                    if k == 0:
                        square_sum[...] = term
                    else:
                        square_sum[...] += term
                else:
                    sums = jnp.dot(
                        weights[...], tensor_t[1 - c, chunk], preferred_element_type=F32
                    )
                    square = square_sum[...] + gram(values, values)
                    sib_send[...] = fold(kept[1 - c] + sums)
                    sib_copy.start()
                    gram_slabs[1 - parity, z] = pack(square)
                    for dz in (2, 1, 3):
                        z_copy(*gram_slab, 1 - parity, dz).start()
                    sums = jnp.dot(weights[...], tensor_t[c, chunk], preferred_element_type=F32)
                    mine[...] = fold(kept[c] + sums)

        for dy, dx in OFFSETS:
            block_copy(dy, dx).wait_send()
        return carry

    lax.fori_loop(0, SWEEPS, sweep, 0)

    anchor_out[:, own_columns] = anchor_own[...]
    anchor_out[:, rows_of(1 - c)] = anchor_sib[...]
    for chunk in range(4):
        dest_out[:, chunk * WIDE : chunk * WIDE + WIDE] = dest[chunk]


def place(anchor_ref, dest_ref, anchor_out, dest_out, sems):
    copies = (
        pltpu.make_async_copy(anchor_ref, anchor_out, sems.at[0]),
        pltpu.make_async_copy(dest_ref, dest_out, sems.at[1]),
    )
    for copy in copies:
        copy.start()
    for copy in copies:
        copy.wait()


def body(counts, block_scales, anchor_factor, dest_factor, hour_factor):
    hbm = pl.BlockSpec(memory_space=pltpu.HBM)
    vmem = pl.BlockSpec(memory_space=pltpu.VMEM)
    dma = pltpu.SemaphoreType.DMA
    columns = dest_factor.shape[1]
    rows = anchor_factor.shape[1]
    small = [
        pltpu.with_memory_space_constraint(value, pltpu.HBM)
        for value in (block_scales, anchor_factor, dest_factor, hour_factor)
    ]
    anchor, dest = pl.pallas_call(
        kernel,
        out_shape=(
            jax.ShapeDtypeStruct((RANK, rows), F32),
            jax.ShapeDtypeStruct((RANK, columns), F32),
        ),
        in_specs=[hbm] * 5,
        out_specs=(vmem, vmem),
        scratch_shapes=[
            pltpu.VMEM((4, 2, HOURS * WIDE, WIDE), BF16),
            pltpu.VMEM((2, 4, HOURS * WIDE, WIDE), BF16),
            pltpu.VMEM((SLOTS, WIDE, 4 * WIDE), jnp.int32),
            pltpu.SMEM((HOURS, 4, 8), F32),
            pltpu.VMEM((HOURS, RANK), F32),
            pltpu.VMEM((2, 2 * RANK, HOURS * WIDE), BF16),
            pltpu.VMEM((4, 2 * RANK, HOURS * WIDE), BF16),
            pltpu.VMEM((HOURS, RANK, WIDE), F32),
            pltpu.VMEM((RANK, RANK), F32),
            pltpu.VMEM((RANK, WIDE), F32),
            pltpu.VMEM((RANK, WIDE), F32),
            pltpu.VMEM((4, RANK, WIDE), F32),
            pltpu.VMEM((RANK, WIDE), F32),
            pltpu.VMEM((RANK, WIDE), F32),
            pltpu.VMEM((RANK, WIDE), F32),
            pltpu.VMEM((RANK, WIDE), F32),
            pltpu.VMEM((16, WIDE), F32),
            pltpu.VMEM((16, WIDE), F32),
            pltpu.VMEM((8, 128), F32),
            pltpu.VMEM((8, 128), F32),
            pltpu.VMEM((2, 4, RANK, WIDE), F32),
            pltpu.VMEM((2, 4, 16, WIDE), F32),
            pltpu.VMEM((4, RANK, WIDE), F32),
            pltpu.VMEM((16, 16, WIDE), F32),
            pltpu.VMEM((32, 128), F32),
            pltpu.VMEM((16, 8, 128), F32),
            pltpu.VMEM((4, 2 * RANK, WIDE), F32),
            pltpu.VMEM((RANK, RANK), F32),
            dma((SLOTS,)),
            dma((7,)),
            dma((6,)),
            dma((2,)),
            dma((4,)),
            dma((2, 4)),
            dma((4,)),
            dma((2, 4)),
            dma((16,)),
            dma((16,)),
            dma((16,)),
            dma((16,)),
            dma((16,)),
            dma((16,)),
        ],
        compiler_params=pltpu.CompilerParams(
            collective_id=0, has_side_effects=True, vmem_limit_bytes=50 * 1024 * 1024
        ),
        name="sweeps",
    )(counts, *small)
    return pl.pallas_call(
        place,
        out_shape=(
            jax.ShapeDtypeStruct((RANK, rows), F32),
            jax.ShapeDtypeStruct((RANK, columns), F32),
        ),
        in_specs=[vmem, vmem],
        out_specs=(hbm, hbm),
        scratch_shapes=[dma((2,))],
        compiler_params=pltpu.CompilerParams(vmem_limit_bytes=2 * 1024 * 1024),
        name="place",
    )(anchor, dest)


def solution(mesh):
    return jax.shard_map(
        body,
        mesh=mesh,
        in_specs=(
            P(None, "org", "dst"),
            P(None, "org", "dst"),
            P(None, "org"),
            P(None, "dst"),
            P(),
        ),
        out_specs=(P(None, "org"), P(None, "dst")),
        check_vma=False,
    )
```

```python
import jax
import jax.numpy as jnp
from jax import lax
from jax.experimental import pallas as pl
from jax.experimental.pallas import tpu as pltpu
from jax.sharding import PartitionSpec as P

RANK = 64
HOURS = 8
SWEEPS = 6
WIDE = 256
SLOTS = 4
MESH = pl.DeviceIdType.MESH
HIGHEST = lax.Precision.HIGHEST
F32 = jnp.float32
BF16 = jnp.bfloat16
FAR = (2, 1, 3, 0)
NEAR = (0, 1, 3, 2)
OFFSETS = sorted(
    [(dy, dx) for dy in range(4) for dx in range(4) if (dy, dx) != (0, 0)],
    key=lambda o: -(min(o[0], 4 - o[0]) + min(o[1], 4 - o[1])),
)


def flip(offset):
    return (4 - offset) % 4


def gram(left, right):
    return lax.dot_general(
        left, right, (((1,), (1,)), ((), ())), precision=HIGHEST, preferred_element_type=F32
    )


def kernel(
    counts_ref, scales_ref, anchor_ref, dest_ref, hour_ref,
    anchor_out, dest_out,
    tensor, tensor_t, stage, scales, hours, weights_a, weights_b, hours_wide, hour_gram,
    anchor_own, anchor_sib, dest, dest_own, mine, sib_send, sib_recv, sib_gram, sib_gram_recv,
    org_gram, org_gram_recv,
    slabs, gram_slabs, partial, parts, gram_send, gram_parts, kept, square_sum,
    stage_sem, in_sem, sib_sems, half_sems, slab_send, slab_recv, gslab_send, gslab_recv,
    part_send, part_recv, gsend, grecv, block_send, block_recv,
):
    o = lax.axis_index("org")
    d = lax.axis_index("dst")
    y, x = o // 4, lax.rem(o, 4)
    z, c = d // 2, lax.rem(d, 2)

    def org_peer(dy, dx):
        return (lax.rem(y + dy, 4) * 4 + lax.rem(x + dx, 4), d)

    def z_peer(dz):
        return (o, lax.rem(z + dz, 4) * 2 + c)

    sibling = (o, z * 2 + 1 - c)

    def rows16(index):
        return pl.ds(pl.multiple_of(index * 16, 16), 16)

    def rows8(index):
        return pl.ds(pl.multiple_of(index * 8, 8), 8)

    def rows_of(hour):
        return pl.ds(pl.multiple_of(hour * WIDE, WIDE), WIDE)

    def stage_copy(step):
        hour, half = lax.rem(step, 8), lax.rem(1 - c + step // 8, 2)
        slot = lax.rem(step, SLOTS)
        return pltpu.make_async_copy(
            counts_ref.at[hour, rows_of(half), :], stage.at[slot], stage_sem.at[slot]
        )

    own_columns = rows_of(c)
    first = [
        pltpu.make_async_copy(scales_ref, scales, in_sem.at[0]),
        pltpu.make_async_copy(hour_ref, hours, in_sem.at[1]),
        pltpu.make_async_copy(anchor_ref.at[:, own_columns], anchor_own, in_sem.at[2]),
    ]
    for chunk in range(4):
        first.append(
            pltpu.make_async_copy(
                dest_ref.at[:, pl.ds(chunk * WIDE, WIDE)], dest.at[chunk], in_sem.at[3 + chunk]
            )
        )
    for copy in first:
        copy.start()
    for step in range(SLOTS):
        stage_copy(step).start()

    barrier = pltpu.get_barrier_semaphore()
    for dy, dx in OFFSETS:
        pl.semaphore_signal(barrier, inc=1, device_id=org_peer(dy, dx), device_id_type=MESH)
    for dz in (1, 2, 3):
        pl.semaphore_signal(barrier, inc=1, device_id=z_peer(dz), device_id_type=MESH)
    pl.semaphore_signal(barrier, inc=1, device_id=sibling, device_id_type=MESH)

    for copy in first:
        copy.wait()

    total = None
    for hour in range(HOURS):
        wide = jnp.broadcast_to(hours[hour : hour + 1, :], (128, RANK)).T
        hours_wide[hour, :, 0:128] = wide
        hours_wide[hour, :, 128:256] = wide
        term = wide[:, 0:RANK] * hours[hour : hour + 1, :]
        total = term if total is None else total + term
    hour_gram[...] = total

    def spread(factor, weights):
        low = factor.astype(BF16).astype(F32)
        for hour in range(HOURS):
            scaled = low * hours_wide[hour]
            high = scaled.astype(BF16)
            rest = (scaled - high.astype(F32)).astype(BF16)
            weights[0:RANK, hour * WIDE : hour * WIDE + WIDE] = high
            weights[RANK : 2 * RANK, hour * WIDE : hour * WIDE + WIDE] = rest

    def fold(sums):
        return sums[0:RANK] + sums[RANK : 2 * RANK]

    def pack(square):
        return jnp.concatenate([square[16 * q : 16 * q + 16] for q in range(4)], axis=1)

    dest_gram = None
    for chunk in range(4):
        spread(dest[chunk], weights_b.at[chunk])
        term = gram(dest[chunk], dest[chunk])
        dest_gram = term if dest_gram is None else dest_gram + term
    dest_own[...] = dest[y]
    gram_slabs[0, z] = pack(dest_gram)
    kept[...] = jnp.zeros_like(kept)

    sib_copy = pltpu.make_async_remote_copy(
        sib_send, sib_recv, sib_sems.at[0], sib_sems.at[1], device_id=sibling, device_id_type=MESH
    )
    sib_gram_copy = pltpu.make_async_remote_copy(
        sib_gram, sib_gram_recv, sib_sems.at[2], sib_sems.at[3],
        device_id=sibling, device_id_type=MESH,
    )
    org_gram_copy = pltpu.make_async_remote_copy(
        org_gram, org_gram_recv, sib_sems.at[4], sib_sems.at[5],
        device_id=sibling, device_id_type=MESH,
    )
    half_copy = pltpu.make_async_remote_copy(
        anchor_own, anchor_sib, half_sems.at[0], half_sems.at[1],
        device_id=sibling, device_id_type=MESH,
    )

    def z_copy(slots, send, recv, parity, dz):
        return pltpu.make_async_remote_copy(
            slots.at[parity, z], slots.at[parity, z], send.at[dz], recv.at[parity, flip(dz)],
            device_id=z_peer(dz), device_id_type=MESH,
        )

    def z_arrival(slots, send, recv, parity, dz):
        where = slots.at[parity, lax.rem(z + dz, 4)]
        return pltpu.make_async_remote_copy(
            where, where, send.at[dz], recv.at[parity, dz],
            device_id=z_peer(dz), device_id_type=MESH,
        )

    slab = (slabs, slab_send, slab_recv)
    gram_slab = (gram_slabs, gslab_send, gslab_recv)

    def load(step, carry):
        hour, half = lax.rem(step, 8), lax.rem(1 - c + step // 8, 2)
        slot = lax.rem(step, SLOTS)
        stage_copy(step).wait()
        for ib in range(2):
            for jb in range(8):
                scale = scales[hour, half * 2 + ib, jb]
                block = stage[slot, ib * 128 : ib * 128 + 128, jb * 128 : jb * 128 + 128]
                values = (block.astype(F32) * scale).astype(BF16)
                row = pl.ds(pl.multiple_of(hour * WIDE + ib * 128, 128), 128)
                tensor[jb // 2, half, row, (jb % 2) * 128 : (jb % 2) * 128 + 128] = values

        @pl.when(step + SLOTS < 2 * HOURS)
        def _():
            stage_copy(step + SLOTS).start()

        sums = kept[step // 8]
        for chunk in range(4):
            sums = sums + lax.dot_general(
                weights_b[chunk, :, rows_of(hour)], tensor[chunk, half, rows_of(hour), :],
                (((1,), (1,)), ((), ())), preferred_element_type=F32,
            )
        kept[step // 8] = sums
        return carry

    lax.fori_loop(0, HOURS, load, 0)
    sib_send[...] = fold(kept[0])
    pl.semaphore_wait(barrier, 19)
    sib_copy.start()
    for dz in (2, 1, 3):
        z_copy(*gram_slab, 0, dz).start()
    lax.fori_loop(HOURS, 2 * HOURS, load, 0)
    mine[...] = fold(kept[1])

    def block_copy(dy, dx):
        where = dest.at[y, rows16(x)]
        return pltpu.make_async_remote_copy(
            where, where, block_send.at[dy * 4 + dx], block_recv.at[flip(dy) * 4 + flip(dx)],
            device_id=org_peer(dy, dx), device_id_type=MESH,
        )

    def block_arrival(dy, dx):
        where = dest.at[lax.rem(y + dy, 4), rows16(lax.rem(x + dx, 4))]
        return pltpu.make_async_remote_copy(
            where, where, block_send.at[dy * 4 + dx], block_recv.at[dy * 4 + dx],
            device_id=org_peer(dy, dx), device_id_type=MESH,
        )

    def part_copy(dy, dx):
        return pltpu.make_async_remote_copy(
            partial.at[dy, rows16(lax.rem(x + dx, 4))], parts.at[flip(dy) * 4 + flip(dx)],
            part_send.at[dy * 4 + dx], part_recv.at[flip(dy) * 4 + flip(dx)],
            device_id=org_peer(dy, dx), device_id_type=MESH,
        )

    def part_arrival(dy, dx):
        return pltpu.make_async_remote_copy(
            partial.at[dy, rows16(lax.rem(x + dx, 4))], parts.at[dy * 4 + dx],
            part_send.at[dy * 4 + dx], part_recv.at[dy * 4 + dx],
            device_id=org_peer(dy, dx), device_id_type=MESH,
        )

    def gram_copy(dy, dx):
        return pltpu.make_async_remote_copy(
            gram_send.at[rows8(lax.rem(x + dx, 4))], gram_parts.at[flip(dy) * 4 + flip(dx)],
            gsend.at[dy * 4 + dx], grecv.at[flip(dy) * 4 + flip(dx)],
            device_id=org_peer(dy, dx), device_id_type=MESH,
        )

    def gram_arrival(dy, dx):
        return pltpu.make_async_remote_copy(
            gram_send.at[rows8(lax.rem(x + dx, 4))], gram_parts.at[dy * 4 + dx],
            gsend.at[dy * 4 + dx], grecv.at[dy * 4 + dx],
            device_id=org_peer(dy, dx), device_id_type=MESH,
        )

    def turn(step, carry):
        half, chunk = lax.rem(step, 2), lax.rem(step // 2, 4)
        hour = rows_of(step // 8)
        tensor_t[half, chunk, hour, :] = tensor[chunk, half, hour, :].T
        return carry

    def sweep(index, carry):
        parity = lax.rem(index, 2)

        sib_copy.wait_recv()
        slabs[parity, z] = mine[...] + sib_recv[...]
        for dz in (2, 1, 3):
            z_copy(*slab, parity, dz).start()
        sib_copy.wait_send()

        @pl.when(index == 0)
        def _():
            lax.fori_loop(0, 4 * HOURS, turn, 0)

        for dz in (1, 3, 2):
            z_arrival(*gram_slab, parity, dz).wait_recv()
        summed = (gram_slabs[parity, 0] + gram_slabs[parity, 1]) + (
            gram_slabs[parity, 2] + gram_slabs[parity, 3]
        )
        sib_gram[...] = summed
        sib_gram_copy.start()
        for dz in (1, 2, 3):
            z_copy(*gram_slab, parity, dz).wait_send()
        sib_gram_copy.wait()
        summed = summed + sib_gram_recv[...]
        square = jnp.concatenate([summed[:, 64 * q : 64 * q + 64] for q in range(4)], axis=0)
        below = jnp.dot(
            square * hour_gram[...], anchor_own[...], precision=HIGHEST, preferred_element_type=F32
        )
        ratio = anchor_own[...] / below
        for dz in (1, 3, 2):
            z_arrival(*slab, parity, dz).wait_recv()
        summed = (slabs[parity, 0] + slabs[parity, 1]) + (slabs[parity, 2] + slabs[parity, 3])
        own = ratio * summed
        anchor_own[...] = own
        half_copy.start()

        anchor_gram = gram(own, own)
        spread(own, weights_a.at[0])
        for q in range(4):
            low, high = 8 * q, 8 * q + 8
            gram_send[low:high, 0:64] = anchor_gram[16 * q : 16 * q + 8]
            gram_send[low:high, 64:128] = anchor_gram[16 * q + 8 : 16 * q + 16]
        for dy, dx in OFFSETS:
            gram_copy(dy, dx).start()
        for dy in FAR:
            kept[dy] = jnp.dot(
                weights_a[0], tensor[lax.rem(y + dy, 4), c], preferred_element_type=F32
            )
        for dz in (1, 2, 3):
            z_copy(*slab, parity, dz).wait_send()
        half_copy.wait()
        other = anchor_sib[...]
        spread(other, weights_a.at[1])
        for dy in FAR:
            sums = kept[dy] + jnp.dot(
                weights_a[1], tensor[lax.rem(y + dy, 4), 1 - c], preferred_element_type=F32
            )
            partial[dy] = fold(sums)
            for dx in FAR:
                if (dy, dx) != (0, 0):
                    part_copy(dy, dx).start()

        @pl.when(index == 0)
        def _():
            lax.fori_loop(4 * HOURS, 8 * HOURS, turn, 0)

        square = gram_send[rows8(x)]
        for dy, dx in reversed(OFFSETS):
            gram_arrival(dy, dx).wait_recv()
            square = square + gram_parts[dy * 4 + dx]
        org_gram[...] = square
        org_gram_copy.start()
        org_gram_copy.wait()
        square = square + org_gram_recv[...]
        square = jnp.concatenate([square[:, 0:64], square[:, 64:128]], axis=0)
        below = jnp.dot(
            square * hour_gram[rows16(x)], dest_own[...],
            precision=HIGHEST, preferred_element_type=F32,
        )
        ratio = dest_own[rows16(x)] / below
        summed = partial[0, rows16(x)]
        for dy, dx in reversed(OFFSETS):
            part_arrival(dy, dx).wait_recv()
            summed = summed + parts[dy * 4 + dx]
        dest[y, rows16(x)] = ratio * summed
        for dy in FAR:
            for dx in FAR:
                if (dy, dx) != (0, 0):
                    block_copy(dy, dx).start()
        for dy, dx in OFFSETS:
            gram_copy(dy, dx).wait_send()
            part_copy(dy, dx).wait_send()

        for k, dy in enumerate(NEAR):
            chunk = lax.rem(y + dy, 4)
            for dx in NEAR:
                if (dy, dx) != (0, 0):
                    block_arrival(dy, dx).wait_recv()

            @pl.when(index < SWEEPS - 1)
            def _():
                values = dest[chunk]
                weights = weights_b.at[k]
                spread(values, weights)
                if dy == 0:
                    dest_own[...] = values
                if k < 3:
                    for half in range(2):
                        sums = jnp.dot(
                            weights[...], tensor_t[half, chunk], preferred_element_type=F32
                        )
                        if k == 0:
                            kept[half] = sums
                        else:
                            kept[half] += sums
                    term = gram(values, values)
                    if k == 0:
                        square_sum[...] = term
                    else:
                        square_sum[...] += term
                else:
                    sums = jnp.dot(
                        weights[...], tensor_t[1 - c, chunk], preferred_element_type=F32
                    )
                    square = square_sum[...] + gram(values, values)
                    sib_send[...] = fold(kept[1 - c] + sums)
                    sib_copy.start()
                    gram_slabs[1 - parity, z] = pack(square)
                    for dz in (2, 1, 3):
                        z_copy(*gram_slab, 1 - parity, dz).start()
                    sums = jnp.dot(weights[...], tensor_t[c, chunk], preferred_element_type=F32)
                    mine[...] = fold(kept[c] + sums)

        for dy, dx in OFFSETS:
            block_copy(dy, dx).wait_send()
        return carry

    lax.fori_loop(0, SWEEPS, sweep, 0)

    anchor_out[:, own_columns] = anchor_own[...]
    anchor_out[:, rows_of(1 - c)] = anchor_sib[...]
    for chunk in range(4):
        dest_out[:, chunk * WIDE : chunk * WIDE + WIDE] = dest[chunk]


def place(anchor_ref, dest_ref, anchor_out, dest_out, sems):
    copies = (
        pltpu.make_async_copy(anchor_ref, anchor_out, sems.at[0]),
        pltpu.make_async_copy(dest_ref, dest_out, sems.at[1]),
    )
    for copy in copies:
        copy.start()
    for copy in copies:
        copy.wait()


def body(counts, block_scales, anchor_factor, dest_factor, hour_factor):
    hbm = pl.BlockSpec(memory_space=pltpu.HBM)
    vmem = pl.BlockSpec(memory_space=pltpu.VMEM)
    dma = pltpu.SemaphoreType.DMA
    columns = dest_factor.shape[1]
    rows = anchor_factor.shape[1]
    small = [
        pltpu.with_memory_space_constraint(value, pltpu.HBM)
        for value in (block_scales, anchor_factor, dest_factor, hour_factor)
    ]
    anchor, dest = pl.pallas_call(
        kernel,
        out_shape=(
            jax.ShapeDtypeStruct((RANK, rows), F32),
            jax.ShapeDtypeStruct((RANK, columns), F32),
        ),
        in_specs=[hbm] * 5,
        out_specs=(vmem, vmem),
        scratch_shapes=[
            pltpu.VMEM((4, 2, HOURS * WIDE, WIDE), BF16),
            pltpu.VMEM((2, 4, HOURS * WIDE, WIDE), BF16),
            pltpu.VMEM((SLOTS, WIDE, 4 * WIDE), jnp.int32),
            pltpu.SMEM((HOURS, 4, 8), F32),
            pltpu.VMEM((HOURS, RANK), F32),
            pltpu.VMEM((2, 2 * RANK, HOURS * WIDE), BF16),
            pltpu.VMEM((4, 2 * RANK, HOURS * WIDE), BF16),
            pltpu.VMEM((HOURS, RANK, WIDE), F32),
            pltpu.VMEM((RANK, RANK), F32),
            pltpu.VMEM((RANK, WIDE), F32),
            pltpu.VMEM((RANK, WIDE), F32),
            pltpu.VMEM((4, RANK, WIDE), F32),
            pltpu.VMEM((RANK, WIDE), F32),
            pltpu.VMEM((RANK, WIDE), F32),
            pltpu.VMEM((RANK, WIDE), F32),
            pltpu.VMEM((RANK, WIDE), F32),
            pltpu.VMEM((16, WIDE), F32),
            pltpu.VMEM((16, WIDE), F32),
            pltpu.VMEM((8, 128), F32),
            pltpu.VMEM((8, 128), F32),
            pltpu.VMEM((2, 4, RANK, WIDE), F32),
            pltpu.VMEM((2, 4, 16, WIDE), F32),
            pltpu.VMEM((4, RANK, WIDE), F32),
            pltpu.VMEM((16, 16, WIDE), F32),
            pltpu.VMEM((32, 128), F32),
            pltpu.VMEM((16, 8, 128), F32),
            pltpu.VMEM((4, 2 * RANK, WIDE), F32),
            pltpu.VMEM((RANK, RANK), F32),
            dma((SLOTS,)),
            dma((7,)),
            dma((6,)),
            dma((2,)),
            dma((4,)),
            dma((2, 4)),
            dma((4,)),
            dma((2, 4)),
            dma((16,)),
            dma((16,)),
            dma((16,)),
            dma((16,)),
            dma((16,)),
            dma((16,)),
        ],
        compiler_params=pltpu.CompilerParams(
            collective_id=0, has_side_effects=True, vmem_limit_bytes=50 * 1024 * 1024
        ),
        name="sweeps",
    )(counts, *small)
    return pl.pallas_call(
        place,
        out_shape=(
            jax.ShapeDtypeStruct((RANK, rows), F32),
            jax.ShapeDtypeStruct((RANK, columns), F32),
        ),
        in_specs=[vmem, vmem],
        out_specs=(hbm, hbm),
        scratch_shapes=[dma((2,))],
        compiler_params=pltpu.CompilerParams(vmem_limit_bytes=2 * 1024 * 1024),
        name="place",
    )(anchor, dest)


def solution(mesh):
    return jax.shard_map(
        body,
        mesh=mesh,
        in_specs=(
            P(None, "org", "dst"),
            P(None, "org", "dst"),
            P(None, "org"),
            P(None, "dst"),
            P(),
        ),
        out_specs=(P(None, "org"), P(None, "dst")),
        check_vma=False,
    )
```
